1024 devices in a mesh: exp: 64 (over y, z_lo, core), rep: 16 (over x, z_hi).
Axes of the slice: x: 4, y: 4, z: 32 (z_hi: 4, z_lo: 8; z = z_hi * 8 + z_lo), core: 2. Of those that a mesh axis runs over, the one named last changes fastest.
Arguments:
- tokens: bfloat16 [8192, 6144], P(('exp', 'rep')), may hold values from -6 to 6
- slot_index: int32 [8192], P(('exp', 'rep')), may hold values from 0 to 2, as said below
- saved_inputs: bfloat16 [16, 512, 6144], P('rep'), may hold values from -6 to 6
- cotangents: bfloat16 [16, 512, 2, 8192], P('rep', None, None, 'exp'), may hold values from -0.046875 to 0.046875
- master: float32 [6144, 2, 8192], P('rep', None, 'exp'), may hold values from -0.078125 to 0.078125
- moment1: float32 [6144, 2, 8192], P('rep', None, 'exp'), may hold values from -0.046875 to 0.046875
- moment2: float32 [6144, 2, 8192], P('rep', None, 'exp'), may hold values from 3e-07 to 3e-05
Outputs:
- new_master: float32 [6144, 2, 8192], P('rep', None, 'exp')
- new_moment1: float32 [6144, 2, 8192], P('rep', None, 'exp')
- new_moment2: float32 [6144, 2, 8192], P('rep', None, 'exp')
- hidden: bfloat16 [16, 128, 8192], P('rep', None, 'exp')
The draws below stay inside these ranges and needn't reach their ends.
Inputs may be any that keep to these rules, and one draw needn't show every extreme that they name: `slot_index`: in each aligned block of 8 tokens every slot 0 to 1 is held by exactly one token; the other tokens carry 2, meaning not routed to this expert.
All inputs are finite; a program needn't handle non-finite values.
Results may differ from the reference program's by a relative error of at most 0.0075.
Values may be sent and summed in bfloat16 or wider, within the bound.
No kernel may reach another device: no remote copies, remote signals or barrier semaphores. Data moves between devices by JAX's collectives and lax.ppermute only.
A program may use at most 64 MiB of HBM per device.

```python
import math
import jax
import jax.numpy as jnp
from jax import lax

D = 6144
FF = 8192
SAVED = 512
TOK_DEV = 8
STEP = 100
CAP = 2
TOKENS = 8192
N_EXP = 64
N_REP = 16


def draw_slot_index(key, part):
    block_count = TOKENS // TOK_DEV
    block_keys = jax.random.split(key, block_count)
    orders = jax.vmap(lambda one_key: jax.random.permutation(one_key, TOK_DEV))(block_keys)
    return jnp.minimum(orders, CAP).astype(jnp.int32).reshape(TOKENS)


def raised(result, own_key, source, target, parts, factor):
    owner, partner = [(jnp.arange(result.shape[dim]) // (result.shape[dim] // parts)).reshape([-1 if axis == dim else 1 for axis in range(result.ndim)]) for dim in (source, target)]
    chosen = jax.random.permutation(own_key, parts)[partner]
    strong = (owner == chosen) | (owner == (partner + parts // 2) % parts)
    return jnp.where(strong, factor * result, result)


def block_scale(key, shape, cuts, smallest, high):
    loudness, own = 1.0, jax.random.fold_in(key, 6)
    for position, shards_of in cuts:
        draws = jnp.exp(jax.random.uniform(jax.random.fold_in(own, position), (shards_of,), jnp.float32, smallest / len(cuts), high / len(cuts)))
        loudness = loudness * jnp.repeat(draws, shape[position] // shards_of).reshape([-1 if axis == position else 1 for axis in range(len(shape))])
    return loudness


def noise(key, dims, width, most, cuts=(), held_as=jnp.bfloat16):
    result = width * jax.random.normal(key, dims, jnp.float32)
    if cuts:
        result = result * block_scale(key, dims, cuts, -0.22, 0.18)
    return jnp.clip(result, -most, most).astype(held_as)


def heavy_noise(own_key, extent, deviation, bound, pieces, heavy, kind=jnp.bfloat16):
    entries = deviation * jax.random.normal(own_key, extent, jnp.float32)
    if pieces:
        entries = entries * block_scale(own_key, extent, pieces, -0.22, 0.18)
    return jnp.clip(raised(entries, jax.random.fold_in(own_key, 3), *heavy), -bound, bound).astype(kind)


def setup_inputs(seed: int = 0) -> dict:
    key_of = jax.random.split(jax.random.key(seed), 8)
    tokens = noise(key_of[0], (TOKENS, D), 1.0, 6.0, ((0, 1024),))
    slot_index = draw_slot_index(jax.random.fold_in(key_of[7], 71), 0)
    saved_inputs = heavy_noise(key_of[2], (N_REP, SAVED, D), 1.0, 6.0, ((0, 16),), (0, 2, 16, 2.0))
    cotangents = noise(key_of[3], (N_REP, SAVED, 2, FF), 0.003, 0.046875, ((0, 16), (3, 64)))
    master = noise(key_of[4], (D, 2, FF), D ** -0.5, 0.078125, ((0, 16), (2, 64)), jnp.float32)
    moment1 = noise(key_of[5], (D, 2, FF), 0.003, 0.046875, ((0, 16), (2, 64)), jnp.float32)
    moment2 = jnp.clip(jnp.exp(math.log(2.9999999242136255e-05) - 4.6051701 * jax.random.uniform(key_of[6], (D, 2, FF), jnp.float32) ** block_scale(key_of[6], (D, 2, FF), ((0, 16), (2, 64)), -0.2, 0.2)), 3.000000106112566e-07, 2.9999999242136255e-05)
    return {"tokens": tokens, "slot_index": slot_index, "saved_inputs": saved_inputs, "cotangents": cotangents, "master": master, "moment1": moment1, "moment2": moment2}


def reference(tokens, slot_index, saved_inputs, cotangents, master, moment1, moment2):

    def add_replica(total, items):
        rows_in, cotangent = items
        part = jnp.dot(rows_in.T, cotangent.reshape(SAVED, 2 * FF), preferred_element_type=jnp.float32)
        rounded = lax.optimization_barrier(part.astype(jnp.bfloat16))
        return (total + rounded.astype(jnp.float32), None)
    total, _ = lax.scan(add_replica, jnp.zeros((D, 2 * FF), jnp.float32), (saved_inputs, cotangents))
    average = (total / N_REP).reshape(D, 2, FF)
    new_first = 0.9 * moment1 + 0.1 * average
    new_second = 0.999 * moment2 + 0.001 * average * average
    correct_one = 1.0 - 0.9 ** STEP
    correct_two = 1.0 - 0.999 ** STEP
    ratio = new_first / correct_one / (jnp.sqrt(new_second / correct_two) + 1e-08)
    new_master = master - 0.001 * (ratio + 0.1 * master)
    weights = new_master.astype(jnp.bfloat16)
    blocks = tokens.reshape(N_EXP, N_REP, TOK_DEV, D).astype(jnp.float32)
    slots = slot_index.reshape(N_EXP, N_REP, TOK_DEV)
    onehot = (slots[:, :, :, None] == jnp.arange(CAP, dtype=jnp.int32)[None, None, None, :]).astype(jnp.float32)
    routed = jnp.einsum('erts,ertd->resd', onehot, blocks).astype(jnp.bfloat16)
    routed = routed.reshape(N_REP * N_EXP * CAP, D)
    preact = jnp.dot(routed, weights.reshape(D, 2 * FF), preferred_element_type=jnp.float32)
    preact = preact.reshape(N_REP * N_EXP * CAP, 2, FF)
    hidden = (jax.nn.silu(preact[:, 0]) * preact[:, 1]).astype(jnp.bfloat16)
    return (new_master, new_first, new_second, hidden.reshape(N_REP, N_EXP * CAP, FF))
```

```python
import functools

import jax
import jax.numpy as jnp
from jax import lax
from jax.experimental import pallas as pl
from jax.experimental.pallas import tpu as pltpu
from jax.sharding import Mesh, PartitionSpec as P


STEP = 100
CAP = 2
bf16, f32 = jnp.bfloat16, jnp.float32


def shift(a, axis, s):
    n = lax.axis_size(axis)
    return lax.ppermute(a, axis, [((i + s) % n, i) for i in range(n)])


def flip(a, axis, bit):
    n = lax.axis_size(axis)
    return lax.ppermute(a, axis, [(i, i ^ bit) for i in range(n)])


def grad_body(n, pos, *refs):
    dims = (((0,), (0,)), ((), ()))
    cot = refs[n]
    for saved, out in zip(refs[:n], refs[n + 1 :]):
        out[0] = lax.dot_general(saved[...], cot[...], dims, preferred_element_type=f32).astype(bf16)


def grad_blocks(pos, saved, cot, width, picks):
    rows, cols = cot.shape

    def source(k, j):
        return lambda i, pos: (0, ((pos[0] + k) & 3) * 4 + ((pos[1] + j + i) & 3))

    n = len(picks)
    return pl.pallas_call(
        functools.partial(grad_body, n),
        grid_spec=pltpu.PrefetchScalarGridSpec(
            num_scalar_prefetch=1,
            grid=(2,),
            in_specs=[pl.BlockSpec((rows, width), source(k, j)) for k, j in picks]
            + [pl.BlockSpec((rows, cols), lambda i, pos: (0, 0))],
            out_specs=[pl.BlockSpec((1, width, cols), lambda i, pos: (i, 0, 0))] * n,
        ),
        out_shape=[jax.ShapeDtypeStruct((2, width, cols), bf16)] * n,
        name="grads",
    )(pos, *[saved] * n, cot)


def pick_body(width, pos, slot, tok, own, near, far):
    t = tok.shape[0]
    row = lax.broadcasted_iota(jnp.int32, (t, 1), 0)
    hits = []
    for s in range(CAP):
        at = 0
        for i in range(t):
            at = at + jnp.where(slot[i] == s, i, 0)
        hits.append(row == at)
    for v, out, base in ((0, own, 0), (1, near, 0), (2, near, CAP), (3, far, 0)):
        for k in range(4):
            block = ((pos[0] + k) & 3) * 4 + (pos[1] ^ v)
            part = tok[:, pl.ds(pl.multiple_of(block * width, width), width)].astype(f32)
            rows = [jnp.sum(jnp.where(hit, part, 0.0), axis=0, keepdims=True) for hit in hits]
            out[base : base + CAP, k * width : (k + 1) * width] = jnp.concatenate(rows, 0).astype(bf16)


def pick(pos, slots, tokens, width):
    smem, vmem = pl.BlockSpec(memory_space=pltpu.SMEM), pl.BlockSpec(memory_space=pltpu.VMEM)
    return pl.pallas_call(
        functools.partial(pick_body, width),
        in_specs=[smem, smem, vmem],
        out_specs=[vmem] * 3,
        out_shape=[jax.ShapeDtypeStruct((n * CAP, 4 * width), bf16) for n in (1, 2, 1)],
        name="pick",
    )(pos, slots, tokens)


def pre_body(where, tok, w0, w1, w2, w3, out):
    width = w0.shape[0]
    acc = None
    for k, w in enumerate((w0, w1, w2, w3)):
        part = jnp.dot(tok[:, k * width : (k + 1) * width], w[...], preferred_element_type=f32)
        acc = part if acc is None else acc + part
    rows = acc.shape[0]
    source = where[...]
    perm = (source == lax.broadcasted_iota(jnp.int32, (rows, rows), 1)).astype(f32).astype(bf16)
    out[...] = jnp.dot(perm, acc.astype(bf16), preferred_element_type=f32).astype(bf16)


def partial_pre(where, tok, ws):
    rows, cols = tok.shape[0], ws[0].shape[1]
    vmem = pl.BlockSpec(memory_space=pltpu.VMEM)
    return pl.pallas_call(
        pre_body,
        in_specs=[vmem] * 6,
        out_specs=vmem,
        out_shape=jax.ShapeDtypeStruct((rows, cols), bf16),
        name="pre",
    )(where, tok, *ws)


def ring_sums(axis, far0, far1, next1, prev0, keep0, keep1):
    got0 = shift(far0, axis, -1)
    got1 = shift(far1, axis, 1)
    own1 = shift(next1, axis, -1)
    own0 = shift(prev0, axis, 1)
    pass0 = (keep0.astype(f32) + got0.astype(f32)).astype(bf16)
    pass1 = (keep1.astype(f32) + got1.astype(f32)).astype(bf16)
    more1 = shift(pass1, axis, 1)
    more0 = shift(pass0, axis, -1)
    return (own0, more0), (own1, more1)


def add(*parts):
    total = parts[0].astype(f32)
    for part in parts[1:]:
        total = total + part.astype(f32)
    return total


def compute(tokens, slot_index, saved_inputs, cotangents, master, moment1, moment2):
    nx, nz = lax.axis_size("x"), lax.axis_size("z_hi")
    ny, nl, nc = lax.axis_size("y"), lax.axis_size("z_lo"), lax.axis_size("core")
    x, z = lax.axis_index("x"), lax.axis_index("z_hi")
    y, low, core = lax.axis_index("y"), lax.axis_index("z_lo"), lax.axis_index("core")
    saved = saved_inputs[0]
    cot = cotangents[0]
    hid = cot.shape[2]
    cols = 2 * hid
    cot = cot.reshape(cot.shape[0], cols)
    width = saved.shape[1] // (nx * nz)

    pos = jnp.stack([x, z]).astype(jnp.int32)

    far0, far1 = grad_blocks(pos, saved, cot, width, [(2, 0), (2, 2)])
    next1, prev0 = grad_blocks(pos, saved, cot, width, [(1, 2), (3, 0)])
    keep0, keep1, mine0, mine1 = grad_blocks(pos, saved, cot, width, [(1, 0), (3, 2), (0, 0), (0, 2)])
    lows, highs = ring_sums("x", far0, far1, next1, prev0, keep0, keep1)
    lows, highs = (mine0,) + lows, (mine1,) + highs
    h = width // 2
    b2 = [add(*[p[0, r] for p in highs]).astype(bf16) for r in (slice(0, h), slice(h, width))]
    b3 = [add(*[p[1, r] for p in highs]).astype(bf16) for r in (slice(0, h), slice(h, width))]
    b0 = add(*[p[0] for p in lows])
    b1 = [add(*[p[1, r] for p in lows]).astype(bf16) for r in (slice(0, h), slice(h, width))]
    first, second = ring_sums("z_hi", b2[0], b2[1], b1[1], b3[0], b1[0], b3[1])
    total = b0 + jnp.concatenate([add(*first), add(*second)], 0)

    own, near, far = pick(pos, slot_index, tokens, width)
    near = flip(near, "z_hi", 1)
    far = flip(jnp.concatenate([far, near[CAP:]], 0), "z_hi", 3)
    tok = jnp.concatenate([own, near[:CAP], far[CAP:], far[:CAP]], 0)[None]
    bit = 1
    while bit < nl:
        tok = jnp.concatenate([tok, flip(tok, "z_lo", bit)], 0)
        bit *= 2
    tok = jnp.concatenate([tok] + [shift(tok, "y", s) for s in range(1, ny)], 0)
    tok = jnp.concatenate([tok] + [shift(tok, "core", s) for s in range(1, nc)], 0)
    tok = tok.reshape(-1, nx * width)

    average = total.reshape(width, 2, hid) / (nx * nz)
    new_first = 0.9 * moment1 + 0.1 * average
    new_second = 0.999 * moment2 + 0.001 * average * average
    correct_one = 1.0 - 0.9**STEP
    correct_two = 1.0 - 0.999**STEP
    ratio = new_first / correct_one / (jnp.sqrt(new_second / correct_two) + 1e-08)
    new_master = master - 0.001 * (ratio + 0.1 * master)
    own_w = new_master.astype(bf16).reshape(width, cols)
    ws = [own_w] + [shift(own_w, "x", s) for s in range(1, nx)]

    row = jnp.arange(tok.shape[0], dtype=jnp.int32)
    slot = row % CAP
    e = (row // CAP) % (ny * nl * nc)
    zt = row // (CAP * ny * nl * nc)
    ec, el, ey = e % nc, (e // nc) % nl, e // (nc * nl)
    held = (((ec - core) % nc) * ny + (ey - y) % ny) * nl + (el ^ low)
    where = held * (nz * CAP) + (zt ^ z) * CAP + slot
    pre = partial_pre(where[:, None], tok, ws).reshape(nz, -1, cols)
    pre = lax.all_to_all(pre, "z_hi", 0, 0, tiled=True)
    pre = jnp.sum(pre.astype(f32), axis=0)
    hidden = (jax.nn.silu(pre[:, :hid]) * pre[:, hid:]).astype(bf16)
    return (new_master, new_first, new_second, hidden[None])


def solution(mesh):
    sizes = (4, 8, 2, 4, 4) if mesh.shape["exp"] == 64 else (2, 4, 2, 4, 4)
    fine = Mesh(mesh.devices.reshape(sizes), ("y", "z_lo", "core", "x", "z_hi"))
    exp, rep = ("y", "z_lo", "core"), ("x", "z_hi")
    return jax.shard_map(
        compute,
        mesh=fine,
        in_specs=(
            P(exp + rep, None),
            P(exp + rep),
            P(rep, None, None),
            P(rep, None, None, exp),
            P(rep, None, exp),
            P(rep, None, exp),
            P(rep, None, exp),
        ),
        out_specs=(
            P(rep, None, exp),
            P(rep, None, exp),
            P(rep, None, exp),
            P(rep, None, exp),
        ),
        check_vma=False,
    )
```

```python
import functools

import jax
import jax.numpy as jnp
from jax import lax
from jax.experimental import pallas as pl
from jax.experimental.pallas import tpu as pltpu
from jax.sharding import Mesh, PartitionSpec as P


STEP = 100
CAP = 2
bf16, f32 = jnp.bfloat16, jnp.float32


def shift(a, axis, s):
    n = lax.axis_size(axis)
    return lax.ppermute(a, axis, [((i + s) % n, i) for i in range(n)])


def flip(a, axis, bit):
    n = lax.axis_size(axis)
    return lax.ppermute(a, axis, [(i, i ^ bit) for i in range(n)])


def grad_body(picks, pos, cot, *refs):
    n = len(picks)
    for saved, out, (_, _, half) in zip(refs[:n], [refs[n + m] for _, m, _ in picks], picks):
        out[half, 0] = jnp.dot(cot[...], saved[...], preferred_element_type=f32).astype(bf16)


def grad_blocks(pos, saved, cot, width, picks):
    cols, rows = cot.shape
    outs = 1 + max(m for _, m, _ in picks)

    def source(k, half):
        return lambda i, pos: (0, ((pos[0] + k) & 3) * 4 + ((pos[1] + 2 * half + i) & 3))

    return pl.pallas_call(
        functools.partial(grad_body, picks),
        grid_spec=pltpu.PrefetchScalarGridSpec(
            num_scalar_prefetch=1,
            grid=(2,),
            in_specs=[pl.BlockSpec((cols, rows), lambda i, pos: (0, 0))]
            + [pl.BlockSpec((rows, width), source(k, half)) for k, _, half in picks],
            out_specs=[pl.BlockSpec((2, 1, cols, width), lambda i, pos: (0, i, 0, 0))] * outs,
        ),
        out_shape=[jax.ShapeDtypeStruct((2, 2, cols, width), bf16)] * outs,
        name="grads",
    )(pos, cot, *[saved] * len(picks))


def pick_body(width, pos, slot, tok, own, near, far):
    t = tok.shape[0]
    row = lax.broadcasted_iota(jnp.int32, (t, 1), 0)
    hits = []
    for s in range(CAP):
        at = 0
        for i in range(t):
            at = at + jnp.where(slot[i] == s, i, 0)
        hits.append(row == at)
    for v, out, base in ((0, own, 0), (1, near, 0), (2, near, CAP), (3, far, 0)):
        for k in range(4):
            block = ((pos[0] + k) & 3) * 4 + (pos[1] ^ v)
            part = tok[:, pl.ds(pl.multiple_of(block * width, width), width)].astype(f32)
            rows = [jnp.sum(jnp.where(hit, part, 0.0), axis=0, keepdims=True) for hit in hits]
            out[base : base + CAP, k * width : (k + 1) * width] = jnp.concatenate(rows, 0).astype(bf16)


def pick(pos, slots, tokens, width):
    smem, vmem = pl.BlockSpec(memory_space=pltpu.SMEM), pl.BlockSpec(memory_space=pltpu.VMEM)
    return pl.pallas_call(
        functools.partial(pick_body, width),
        in_specs=[smem, smem, vmem],
        out_specs=[vmem] * 3,
        out_shape=[jax.ShapeDtypeStruct((n * CAP, 4 * width), bf16) for n in (1, 2, 1)],
        name="pick",
    )(pos, slots, tokens)


def pre_body(where, tok, w0, w1, w2, w3, out):
    width = w0.shape[0]
    acc = None
    for k, w in enumerate((w0, w1, w2, w3)):
        part = jnp.dot(tok[:, k * width : (k + 1) * width], w[...], preferred_element_type=f32)
        acc = part if acc is None else acc + part
    rows = acc.shape[0]
    source = where[...]
    perm = (source == lax.broadcasted_iota(jnp.int32, (rows, rows), 1)).astype(f32).astype(bf16)
    out[...] = jnp.dot(perm, acc.astype(bf16), preferred_element_type=f32).astype(bf16)


def partial_pre(where, tok, ws):
    rows, cols = tok.shape[0], ws[0].shape[1]
    vmem = pl.BlockSpec(memory_space=pltpu.VMEM)
    return pl.pallas_call(
        pre_body,
        in_specs=[vmem] * 6,
        out_specs=vmem,
        out_shape=jax.ShapeDtypeStruct((rows, cols), bf16),
        name="pre",
    )(where, tok, *ws)


def ring_sums(axis, far0, far1, next1, prev0, keep0, keep1):
    got0 = shift(far0, axis, -1)
    got1 = shift(far1, axis, 1)
    own1 = shift(next1, axis, -1)
    own0 = shift(prev0, axis, 1)
    return pass_on(axis, got0, got1, own0, own1, keep0, keep1)


def pass_on(axis, got0, got1, own0, own1, keep0, keep1):
    pass0 = add(keep0, got0).astype(bf16)
    pass1 = add(keep1, got1).astype(bf16)
    more1 = shift(pass1, axis, 1)
    more0 = shift(pass0, axis, -1)
    return (own0, more0), (own1, more1)


def add(*parts):
    total = parts[0].astype(f32)
    for part in parts[1:]:
        total = total + part.astype(f32)
    return total


def compute(tokens, slot_index, saved_inputs, cotangents, master, moment1, moment2):
    nx, nz = lax.axis_size("x"), lax.axis_size("z_hi")
    ny, nl, nc = lax.axis_size("y"), lax.axis_size("z_lo"), lax.axis_size("core")
    x, z = lax.axis_index("x"), lax.axis_index("z_hi")
    y, low, core = lax.axis_index("y"), lax.axis_index("z_lo"), lax.axis_index("core")
    saved = saved_inputs[0]
    cot = cotangents[0]
    hid = cot.shape[2]
    cols = 2 * hid
    cot = cot.reshape(cot.shape[0], cols).T
    width = saved.shape[1] // (nx * nz)

    pos = jnp.stack([x, z]).astype(jnp.int32)

    to_next, to_prev = grad_blocks(pos, saved, cot, width, [(2, 0, 0), (1, 0, 1), (3, 1, 0), (2, 1, 1)])
    keep, mine = grad_blocks(pos, saved, cot, width, [(1, 0, 0), (3, 0, 1), (0, 1, 0), (0, 1, 1)])
    got = shift(to_next, "x", -1), shift(to_prev, "x", 1)
    lows, highs = pass_on("x", got[0][0], got[1][1], got[1][0], got[0][1], keep[0], keep[1])
    lows, highs = (mine[0],) + lows, (mine[1],) + highs
    gate, up = slice(0, hid), slice(hid, cols)
    b2 = [add(*[p[0, r] for p in highs]).astype(bf16) for r in (gate, up)]
    b3 = [add(*[p[1, r] for p in highs]).astype(bf16) for r in (gate, up)]
    b0 = add(*[p[0] for p in lows])
    b1 = [add(*[p[1, r] for p in lows]).astype(bf16) for r in (gate, up)]
    first, second = ring_sums("z_hi", b2[0], b2[1], b1[1], b3[0], b1[0], b3[1])
    total = jnp.stack([add(b0[gate], *first).T, add(b0[up], *second).T], axis=1)

    own, near, far = pick(pos, slot_index, tokens, width)
    near = flip(near, "z_hi", 1)
    far = flip(jnp.concatenate([far, near[CAP:]], 0), "z_hi", 3)
    tok = jnp.concatenate([own, near[:CAP], far[CAP:], far[:CAP]], 0)[None]
    bit = 1
    while bit < nl:
        tok = jnp.concatenate([tok, flip(tok, "z_lo", bit)], 0)
        bit *= 2
    tok = jnp.concatenate([tok, flip(tok, "y", 1)], 0)
    tok = jnp.concatenate([tok, flip(tok, "y", 3)], 0)
    tok = jnp.concatenate([tok] + [shift(tok, "core", s) for s in range(1, nc)], 0)
    tok = tok.reshape(-1, nx * width)

    average = total / (nx * nz)
    new_first = 0.9 * moment1 + 0.1 * average
    new_second = 0.999 * moment2 + 0.001 * average * average
    correct_one = 1.0 - 0.9**STEP
    correct_two = 1.0 - 0.999**STEP
    ratio = new_first / correct_one / (jnp.sqrt(new_second / correct_two) + 1e-08)
    new_master = master - 0.001 * (ratio + 0.1 * master)
    own_w = new_master.astype(bf16).reshape(width, cols)
    ws = [own_w] + [shift(own_w, "x", s) for s in range(1, nx)]

    row = jnp.arange(tok.shape[0], dtype=jnp.int32)
    slot = row % CAP
    e = (row // CAP) % (ny * nl * nc)
    zt = row // (CAP * ny * nl * nc)
    ec, el, ey = e % nc, (e // nc) % nl, e // (nc * nl)
    dy = ey ^ y
    held = (((ec - core) % nc) * ny + (dy ^ (dy >> 1))) * nl + (el ^ low)
    where = held * (nz * CAP) + (zt ^ z) * CAP + slot
    pre = partial_pre(where[:, None], tok, ws).reshape(nz, -1, cols)
    pre = lax.all_to_all(pre, "z_hi", 0, 0, tiled=True)
    pre = jnp.sum(pre.astype(f32), axis=0)
    hidden = (jax.nn.silu(pre[:, :hid]) * pre[:, hid:]).astype(bf16)
    return (new_master, new_first, new_second, hidden[None])


def solution(mesh):
    sizes = (4, 8, 2, 4, 4) if mesh.shape["exp"] == 64 else (2, 4, 2, 4, 4)
    fine = Mesh(mesh.devices.reshape(sizes), ("y", "z_lo", "core", "x", "z_hi"))
    exp, rep = ("y", "z_lo", "core"), ("x", "z_hi")
    return jax.shard_map(
        compute,
        mesh=fine,
        in_specs=(
            P(exp + rep, None),
            P(exp + rep),
            P(rep, None, None),
            P(rep, None, None, exp),
            P(rep, None, exp),
            P(rep, None, exp),
            P(rep, None, exp),
        ),
        out_specs=(
            P(rep, None, exp),
            P(rep, None, exp),
            P(rep, None, exp),
            P(rep, None, exp),
        ),
        check_vma=False,
    )
```

```python
import functools

import jax
import jax.numpy as jnp
from jax import lax
from jax.experimental import pallas as pl
from jax.experimental.pallas import tpu as pltpu
from jax.sharding import Mesh, PartitionSpec as P


STEP = 100
CAP = 2
bf16, f32 = jnp.bfloat16, jnp.float32


def shift(a, axis, s):
    n = lax.axis_size(axis)
    return lax.ppermute(a, axis, [((i + s) % n, i) for i in range(n)])


def flip(a, axis, bit):
    n = lax.axis_size(axis)
    return lax.ppermute(a, axis, [(i, i ^ bit) for i in range(n)])


def grad_body(picks, pos, cot, *refs):
    n = len(picks)
    for saved, (_, m, half) in zip(refs[:n], picks):
        block = lax.dot_general(saved[...], cot[...], (((0,), (0,)), ((), ())), preferred_element_type=f32)
        refs[n + m][half, 0] = block.astype(bf16)


def grad_blocks(pos, saved, cot, width, picks):
    rows, cols = cot.shape
    outs = 1 + max(m for _, m, _ in picks)

    def source(k, half):
        return lambda i, pos: (0, ((pos[0] + k) & 3) * 4 + 2 * half + i)

    return pl.pallas_call(
        functools.partial(grad_body, picks),
        grid_spec=pltpu.PrefetchScalarGridSpec(
            num_scalar_prefetch=1,
            grid=(2,),
            in_specs=[pl.BlockSpec((rows, cols), lambda i, pos: (0, 0))]
            + [pl.BlockSpec((rows, width), source(k, half)) for k, _, half in picks],
            out_specs=[pl.BlockSpec((2, 1, width, cols), lambda i, pos: (0, i, 0, 0))] * outs,
        ),
        out_shape=[jax.ShapeDtypeStruct((2, 2, width, cols), bf16)] * outs,
        name="grads",
    )(pos, cot, *[saved] * len(picks))


def pick_body(width, pos, slot, tok, own, near, far):
    t = tok.shape[0]
    row = lax.broadcasted_iota(jnp.int32, (t, 1), 0)
    hits = []
    for s in range(CAP):
        at = 0
        for i in range(t):
            at = at + jnp.where(slot[i] == s, i, 0)
        hits.append(row == at)
    for v, out, base in ((0, own, 0), (1, near, 0), (2, near, CAP), (3, far, 0)):
        for k in range(4):
            block = ((pos[0] + k) & 3) * 4 + (pos[1] ^ v)
            part = tok[:, pl.ds(pl.multiple_of(block * width, width), width)].astype(f32)
            rows = [jnp.sum(jnp.where(hit, part, 0.0), axis=0, keepdims=True) for hit in hits]
            out[base : base + CAP, k * width : (k + 1) * width] = jnp.concatenate(rows, 0).astype(bf16)


def pick(pos, slots, tokens, width):
    smem, vmem = pl.BlockSpec(memory_space=pltpu.SMEM), pl.BlockSpec(memory_space=pltpu.VMEM)
    return pl.pallas_call(
        functools.partial(pick_body, width),
        in_specs=[smem, smem, vmem],
        out_specs=[vmem] * 3,
        out_shape=[jax.ShapeDtypeStruct((n * CAP, 4 * width), bf16) for n in (1, 2, 1)],
        name="pick",
    )(pos, slots, tokens)


def pre_body(where, tok, w0, w1, w2, w3, out):
    width = w0.shape[0]
    acc = None
    for k, w in enumerate((w0, w1, w2, w3)):
        part = jnp.dot(tok[:, k * width : (k + 1) * width], w[...], preferred_element_type=f32)
        acc = part if acc is None else acc + part
    rows = acc.shape[0]
    source = where[...]
    perm = (source == lax.broadcasted_iota(jnp.int32, (rows, rows), 1)).astype(f32).astype(bf16)
    out[...] = jnp.dot(perm, acc.astype(bf16), preferred_element_type=f32).astype(bf16)


def partial_pre(where, tok, ws):
    rows, cols = tok.shape[0], ws[0].shape[1]
    vmem = pl.BlockSpec(memory_space=pltpu.VMEM)
    return pl.pallas_call(
        pre_body,
        in_specs=[vmem] * 6,
        out_specs=vmem,
        out_shape=jax.ShapeDtypeStruct((rows, cols), bf16),
        name="pre",
    )(where, tok, *ws)


def ring_sums(axis, to_next, to_prev, keep, mine):
    from_prev = shift(to_next, axis, -1)
    from_next = shift(to_prev, axis, 1)
    pass0 = add(keep[0], from_prev[0]).astype(bf16)
    pass1 = add(keep[1], from_next[1]).astype(bf16)
    more1 = shift(pass1, axis, 1)
    more0 = shift(pass0, axis, -1)
    halves = add(mine[0], from_next[0], more0), add(mine[1], from_prev[1], more1)
    return jnp.concatenate([half.astype(bf16) for half in halves], 0)


def add(*parts):
    total = parts[0].astype(f32)
    for part in parts[1:]:
        total = total + part.astype(f32)
    return total


def compute(tokens, slot_index, saved_inputs, cotangents, master, moment1, moment2):
    nx, nz = lax.axis_size("x"), lax.axis_size("z_hi")
    ny, nl, nc = lax.axis_size("y"), lax.axis_size("z_lo"), lax.axis_size("core")
    x, z = lax.axis_index("x"), lax.axis_index("z_hi")
    y, low, core = lax.axis_index("y"), lax.axis_index("z_lo"), lax.axis_index("core")
    saved = saved_inputs[0]
    cot = cotangents[0]
    hid = cot.shape[2]
    cols = 2 * hid
    cot = cot.reshape(cot.shape[0], cols)
    width = saved.shape[1] // (nx * nz)

    pos = jnp.stack([x, z]).astype(jnp.int32)

    to_next, to_prev = grad_blocks(pos, saved, cot, width, [(2, 0, 0), (1, 0, 1), (3, 1, 0), (2, 1, 1)])
    keep, mine = grad_blocks(pos, saved, cot, width, [(1, 0, 0), (3, 0, 1), (0, 1, 0), (0, 1, 1)])
    half_sum = ring_sums("x", to_next, to_prev, keep, mine)

    own, near, far = pick(pos, slot_index, tokens, width)
    near = flip(near, "z_hi", 1)
    far, near, half_sum = lax.optimization_barrier((far, near, half_sum))
    far = flip(jnp.concatenate([far, near[CAP:]], 0), "z_hi", 3)
    tok = jnp.concatenate([own, near[:CAP], far[CAP:], far[:CAP]], 0)[None]
    bit = 1
    while bit < nl:
        tok = jnp.concatenate([tok, flip(tok, "z_lo", bit)], 0)
        bit *= 2
    tok = jnp.concatenate([tok, flip(tok, "y", 1)], 0)
    tok = jnp.concatenate([tok, flip(tok, "y", 3)], 0)
    tok = jnp.concatenate([tok] + [shift(tok, "core", s) for s in range(1, nc)], 0)
    tok = tok.reshape(-1, nx * width)

    total = lax.psum_scatter(half_sum.reshape(-1, cols), "z_hi", scatter_dimension=0, tiled=True).astype(f32)
    average = total.reshape(width, 2, hid) / (nx * nz)
    new_first = 0.9 * moment1 + 0.1 * average
    new_second = 0.999 * moment2 + 0.001 * average * average
    correct_one = 1.0 - 0.9**STEP
    correct_two = 1.0 - 0.999**STEP
    ratio = new_first / correct_one / (jnp.sqrt(new_second / correct_two) + 1e-08)
    new_master = master - 0.001 * (ratio + 0.1 * master)
    own_w = new_master.astype(bf16).reshape(width, cols)
    ws = [own_w] + [shift(own_w, "x", s) for s in range(1, nx)]

    row = jnp.arange(tok.shape[0], dtype=jnp.int32)
    slot = row % CAP
    e = (row // CAP) % (ny * nl * nc)
    zt = row // (CAP * ny * nl * nc)
    ec, el, ey = e % nc, (e // nc) % nl, e // (nc * nl)
    dy = ey ^ y
    held = (((ec - core) % nc) * ny + (dy ^ (dy >> 1))) * nl + (el ^ low)
    where = held * (nz * CAP) + (zt ^ z) * CAP + slot
    pre = partial_pre(where[:, None], tok, ws).reshape(nz, -1, cols)
    pre = lax.all_to_all(pre, "z_hi", 0, 0, tiled=True)
    pre = jnp.sum(pre.astype(f32), axis=0)
    hidden = (jax.nn.silu(pre[:, :hid]) * pre[:, hid:]).astype(bf16)
    return (new_master, new_first, new_second, hidden[None])


def solution(mesh):
    sizes = (4, 8, 2, 4, 4) if mesh.shape["exp"] == 64 else (2, 4, 2, 4, 4)
    fine = Mesh(mesh.devices.reshape(sizes), ("y", "z_lo", "core", "x", "z_hi"))
    exp, rep = ("y", "z_lo", "core"), ("x", "z_hi")
    return jax.shard_map(
        compute,
        mesh=fine,
        in_specs=(
            P(exp + rep, None),
            P(exp + rep),
            P(rep, None, None),
            P(rep, None, None, exp),
            P(rep, None, exp),
            P(rep, None, exp),
            P(rep, None, exp),
        ),
        out_specs=(
            P(rep, None, exp),
            P(rep, None, exp),
            P(rep, None, exp),
            P(rep, None, exp),
        ),
        check_vma=False,
    )
```

```python
import functools

import jax
import jax.numpy as jnp
from jax import lax
from jax.experimental import pallas as pl
from jax.experimental.pallas import tpu as pltpu
from jax.sharding import Mesh, PartitionSpec as P


STEP = 100
CAP = 2
bf16, f32 = jnp.bfloat16, jnp.float32


def shift(a, axis, s):
    n = lax.axis_size(axis)
    return lax.ppermute(a, axis, [((i + s) % n, i) for i in range(n)])


def flip(a, axis, bit):
    n = lax.axis_size(axis)
    return lax.ppermute(a, axis, [(i, i ^ bit) for i in range(n)])


def grad_body(picks, pos, cot, *refs):
    n = len(picks)
    for saved, (_, m, half) in zip(refs[:n], picks):
        block = lax.dot_general(saved[...], cot[...], (((0,), (0,)), ((), ())), preferred_element_type=f32)
        refs[n + m][half, 0] = block.astype(bf16)


def grad_blocks(pos, saved, cot, width, picks):
    rows, cols = cot.shape
    outs = 1 + max(m for _, m, _ in picks)

    def source(k, half):
        return lambda i, pos: (0, ((pos[0] + k) & 3) * 4 + 2 * half + i)

    return pl.pallas_call(
        functools.partial(grad_body, picks),
        grid_spec=pltpu.PrefetchScalarGridSpec(
            num_scalar_prefetch=1,
            grid=(2,),
            in_specs=[pl.BlockSpec((rows, cols), lambda i, pos: (0, 0))]
            + [pl.BlockSpec((rows, width), source(k, half)) for k, _, half in picks],
            out_specs=[pl.BlockSpec((2, 1, width, cols), lambda i, pos: (0, i, 0, 0))] * outs,
        ),
        out_shape=[jax.ShapeDtypeStruct((2, 2, width, cols), bf16)] * outs,
        name="grads",
    )(pos, cot, *[saved] * len(picks))


def pick_body(width, pos, slot, tok, own, near, far):
    t = tok.shape[0]
    row = lax.broadcasted_iota(jnp.int32, (t, 1), 0)
    hits = []
    for s in range(CAP):
        at = 0
        for i in range(t):
            at = at + jnp.where(slot[i] == s, i, 0)
        hits.append(row == at)
    for v, out, base in ((0, own, 0), (1, near, 0), (2, near, CAP), (3, far, 0)):
        for k in range(4):
            block = ((pos[0] + k) & 3) * 4 + (pos[1] ^ v)
            part = tok[:, pl.ds(pl.multiple_of(block * width, width), width)].astype(f32)
            rows = [jnp.sum(jnp.where(hit, part, 0.0), axis=0, keepdims=True) for hit in hits]
            out[base : base + CAP, k * width : (k + 1) * width] = jnp.concatenate(rows, 0).astype(bf16)


def pick(pos, slots, tokens, width):
    smem, vmem = pl.BlockSpec(memory_space=pltpu.SMEM), pl.BlockSpec(memory_space=pltpu.VMEM)
    return pl.pallas_call(
        functools.partial(pick_body, width),
        in_specs=[smem, smem, vmem],
        out_specs=[vmem] * 3,
        out_shape=[jax.ShapeDtypeStruct((n * CAP, 4 * width), bf16) for n in (1, 2, 1)],
        name="pick",
    )(pos, slots, tokens)


def pre_body(where, tok, w0, w1, w2, w3, out):
    width = w0.shape[0]
    acc = None
    for k, w in enumerate((w0, w1, w2, w3)):
        part = jnp.dot(tok[:, k * width : (k + 1) * width], w[...], preferred_element_type=f32)
        acc = part if acc is None else acc + part
    rows = acc.shape[0]
    source = where[...]
    perm = (source == lax.broadcasted_iota(jnp.int32, (rows, rows), 1)).astype(f32).astype(bf16)
    out[...] = jnp.dot(perm, acc.astype(bf16), preferred_element_type=f32).astype(bf16)


def partial_pre(where, tok, ws):
    rows, cols = tok.shape[0], ws[0].shape[1]
    vmem = pl.BlockSpec(memory_space=pltpu.VMEM)
    return pl.pallas_call(
        pre_body,
        in_specs=[vmem] * 6,
        out_specs=vmem,
        out_shape=jax.ShapeDtypeStruct((rows, cols), bf16),
        name="pre",
    )(where, tok, *ws)


def ring_sums(axis, to_next, to_prev, keep, mine):
    from_prev = shift(to_next, axis, -1)
    from_next = shift(to_prev, axis, 1)
    pass0 = add(keep[0], from_prev[0]).astype(bf16)
    pass1 = add(keep[1], from_next[1]).astype(bf16)
    more1 = shift(pass1, axis, 1)
    more0 = shift(pass0, axis, -1)
    halves = add(mine[0], from_next[0], more0), add(mine[1], from_prev[1], more1)
    return jnp.concatenate([half.astype(bf16) for half in halves], 0)


def add(*parts):
    total = parts[0].astype(f32)
    for part in parts[1:]:
        total = total + part.astype(f32)
    return total


def compute(tokens, slot_index, saved_inputs, cotangents, master, moment1, moment2):
    nx, nz = lax.axis_size("x"), lax.axis_size("z_hi")
    ny, nl, nc = lax.axis_size("y"), lax.axis_size("z_lo"), lax.axis_size("core")
    x, z = lax.axis_index("x"), lax.axis_index("z_hi")
    y, low, core = lax.axis_index("y"), lax.axis_index("z_lo"), lax.axis_index("core")
    saved = saved_inputs[0]
    cot = cotangents[0]
    hid = cot.shape[2]
    cols = 2 * hid
    cot = cot.reshape(cot.shape[0], cols)
    width = saved.shape[1] // (nx * nz)

    pos = jnp.stack([x, z]).astype(jnp.int32)

    to_next, to_prev = grad_blocks(pos, saved, cot, width, [(2, 0, 0), (1, 0, 1), (3, 1, 0), (2, 1, 1)])
    keep, mine = grad_blocks(pos, saved, cot, width, [(1, 0, 0), (3, 0, 1), (0, 1, 0), (0, 1, 1)])
    half_sum = ring_sums("x", to_next, to_prev, keep, mine)

    own, near, far = pick(pos, slot_index, tokens, width)
    near = flip(near, "z_hi", 1)
    far, near, half_sum = lax.optimization_barrier((far, near, half_sum))
    far = flip(jnp.concatenate([far, near[CAP:]], 0), "z_hi", 3)
    tok = jnp.concatenate([own, near[:CAP], far[CAP:], far[:CAP]], 0)[None]
    for bit in (4, 2, 1):
        tok = jnp.concatenate([tok, flip(tok, "z_lo", bit)], 0)
    tok = jnp.concatenate([tok] + [shift(tok, "y", s) for s in range(1, ny)], 0)
    tok = jnp.concatenate([tok] + [shift(tok, "core", s) for s in range(1, nc)], 0)
    tok = tok.reshape(-1, nx * width)

    total = lax.psum_scatter(half_sum.reshape(-1, cols), "z_hi", scatter_dimension=0, tiled=True).astype(f32)
    average = total.reshape(width, 2, hid) / (nx * nz)
    new_first = 0.9 * moment1 + 0.1 * average
    new_second = 0.999 * moment2 + 0.001 * average * average
    correct_one = 1.0 - 0.9**STEP
    correct_two = 1.0 - 0.999**STEP
    ratio = new_first / correct_one / (jnp.sqrt(new_second / correct_two) + 1e-08)
    new_master = master - 0.001 * (ratio + 0.1 * master)
    own_w = new_master.astype(bf16).reshape(width, cols)
    ws = [own_w] + [shift(own_w, "x", s) for s in range(1, nx)]

    row = jnp.arange(tok.shape[0], dtype=jnp.int32)
    slot = row % CAP
    e = (row // CAP) % (ny * nl * nc)
    zt = row // (CAP * ny * nl * nc)
    ec, el, ey = e % nc, (e // nc) % nl, e // (nc * nl)
    dl = el ^ low
    dl = (dl >> 2) + (dl & 2) + 4 * (dl & 1)
    held = (((ec - core) % nc) * ny + (ey - y) % ny) * nl + dl
    where = held * (nz * CAP) + (zt ^ z) * CAP + slot
    pre = partial_pre(where[:, None], tok, ws).reshape(nz, -1, cols)
    pre = lax.all_to_all(pre, "z_hi", 0, 0, tiled=True)
    pre = jnp.sum(pre.astype(f32), axis=0)
    hidden = (jax.nn.silu(pre[:, :hid]) * pre[:, hid:]).astype(bf16)
    return (new_master, new_first, new_second, hidden[None])


def solution(mesh):
    sizes = (4, 8, 2, 4, 4) if mesh.shape["exp"] == 64 else (2, 4, 2, 4, 4)
    fine = Mesh(mesh.devices.reshape(sizes), ("y", "z_lo", "core", "x", "z_hi"))
    exp, rep = ("y", "z_lo", "core"), ("x", "z_hi")
    return jax.shard_map(
        compute,
        mesh=fine,
        in_specs=(
            P(exp + rep, None),
            P(exp + rep),
            P(rep, None, None),
            P(rep, None, None, exp),
            P(rep, None, exp),
            P(rep, None, exp),
            P(rep, None, exp),
        ),
        out_specs=(
            P(rep, None, exp),
            P(rep, None, exp),
            P(rep, None, exp),
            P(rep, None, exp),
        ),
        check_vma=False,
    )
```

```python
import functools

import jax
import jax.numpy as jnp
from jax import lax
from jax.experimental import pallas as pl
from jax.experimental.pallas import tpu as pltpu
from jax.sharding import Mesh, PartitionSpec as P


STEP = 100
CAP = 2
bf16, f32 = jnp.bfloat16, jnp.float32


def shift(a, axis, s):
    n = lax.axis_size(axis)
    return lax.ppermute(a, axis, [((i + s) % n, i) for i in range(n)])


def flip(a, axis, bit):
    n = lax.axis_size(axis)
    return lax.ppermute(a, axis, [(i, i ^ bit) for i in range(n)])


def grad_body(picks, pos, cot, *refs):
    n = len(picks)
    for saved, (_, m, half) in zip(refs[:n], picks):
        block = lax.dot_general(saved[...], cot[...], (((0,), (0,)), ((), ())), preferred_element_type=f32)
        refs[n + m][half, 0] = block.astype(bf16)


def grad_blocks(pos, saved, cot, width, picks):
    rows, cols = cot.shape
    outs = 1 + max(m for _, m, _ in picks)

    def source(k, half):
        return lambda i, pos: (0, ((pos[0] + k) & 3) * 4 + ((pos[1] + 2 * half + i) & 3))

    return pl.pallas_call(
        functools.partial(grad_body, picks),
        grid_spec=pltpu.PrefetchScalarGridSpec(
            num_scalar_prefetch=1,
            grid=(2,),
            in_specs=[pl.BlockSpec((rows, cols), lambda i, pos: (0, 0))]
            + [pl.BlockSpec((rows, width), source(k, half)) for k, _, half in picks],
            out_specs=[pl.BlockSpec((2, 1, width, cols), lambda i, pos: (0, i, 0, 0))] * outs,
        ),
        out_shape=[jax.ShapeDtypeStruct((2, 2, width, cols), bf16)] * outs,
        name="grads",
    )(pos, cot, *[saved] * len(picks))


def pick_body(width, pos, slot, tok, own, near, far):
    t = tok.shape[0]
    row = lax.broadcasted_iota(jnp.int32, (t, 1), 0)
    hits = []
    for s in range(CAP):
        at = 0
        for i in range(t):
            at = at + jnp.where(slot[i] == s, i, 0)
        hits.append(row == at)
    for v, out, base in ((0, own, 0), (1, near, 0), (2, near, CAP), (3, far, 0)):
        for k in range(4):
            block = ((pos[0] + k) & 3) * 4 + (pos[1] ^ v)
            part = tok[:, pl.ds(pl.multiple_of(block * width, width), width)].astype(f32)
            rows = [jnp.sum(jnp.where(hit, part, 0.0), axis=0, keepdims=True) for hit in hits]
            out[base : base + CAP, k * width : (k + 1) * width] = jnp.concatenate(rows, 0).astype(bf16)


def pick(pos, slots, tokens, width):
    smem, vmem = pl.BlockSpec(memory_space=pltpu.SMEM), pl.BlockSpec(memory_space=pltpu.VMEM)
    return pl.pallas_call(
        functools.partial(pick_body, width),
        in_specs=[smem, smem, vmem],
        out_specs=[vmem] * 3,
        out_shape=[jax.ShapeDtypeStruct((n * CAP, 4 * width), bf16) for n in (1, 2, 1)],
        name="pick",
    )(pos, slots, tokens)


def pre_body(where, tok, w0, w1, w2, w3, out):
    width = w0.shape[0]
    acc = None
    for k, w in enumerate((w0, w1, w2, w3)):
        part = jnp.dot(tok[:, k * width : (k + 1) * width], w[...], preferred_element_type=f32)
        acc = part if acc is None else acc + part
    rows = acc.shape[0]
    source = where[...]
    perm = (source == lax.broadcasted_iota(jnp.int32, (rows, rows), 1)).astype(f32).astype(bf16)
    out[...] = jnp.dot(perm, acc.astype(bf16), preferred_element_type=f32).astype(bf16)


def partial_pre(where, tok, ws):
    rows, cols = tok.shape[0], ws[0].shape[1]
    vmem = pl.BlockSpec(memory_space=pltpu.VMEM)
    return pl.pallas_call(
        pre_body,
        in_specs=[vmem] * 6,
        out_specs=vmem,
        out_shape=jax.ShapeDtypeStruct((rows, cols), bf16),
        name="pre",
    )(where, tok, *ws)


def ring_sums(axis, to_next, to_prev, keep, mine):
    from_prev = shift(to_next, axis, -1)
    from_next = shift(to_prev, axis, 1)
    pass0 = add(keep[0], from_prev[0]).astype(bf16)
    pass1 = add(keep[1], from_next[1]).astype(bf16)
    more1 = shift(pass1, axis, 1)
    more0 = shift(pass0, axis, -1)
    return add(mine[0], from_next[0], more0), add(mine[1], from_prev[1], more1)


def add(*parts):
    total = parts[0].astype(f32)
    for part in parts[1:]:
        total = total + part.astype(f32)
    return total


def compute(tokens, slot_index, saved_inputs, cotangents, master, moment1, moment2):
    nx, nz = lax.axis_size("x"), lax.axis_size("z_hi")
    ny, nl, nc = lax.axis_size("y"), lax.axis_size("z_lo"), lax.axis_size("core")
    x, z = lax.axis_index("x"), lax.axis_index("z_hi")
    y, low, core = lax.axis_index("y"), lax.axis_index("z_lo"), lax.axis_index("core")
    saved = saved_inputs[0]
    cot = cotangents[0]
    hid = cot.shape[2]
    cols = 2 * hid
    cot = cot.reshape(cot.shape[0], cols)
    width = saved.shape[1] // (nx * nz)

    pos = jnp.stack([x, z]).astype(jnp.int32)

    to_next, to_prev = grad_blocks(pos, saved, cot, width, [(2, 0, 0), (1, 0, 1), (3, 1, 0), (2, 1, 1)])
    keep, mine = grad_blocks(pos, saved, cot, width, [(1, 0, 0), (3, 0, 1), (0, 1, 0), (0, 1, 1)])
    near_sum, far_sum = ring_sums("x", to_next, to_prev, keep, mine)
    h = width // 2
    b0, b1 = near_sum[0], near_sum[1].astype(bf16)
    b2, b3 = far_sum[0].astype(bf16), far_sum[1].astype(bf16)
    to_next, to_prev = jnp.stack([b2[:h], b1[h:]]), jnp.stack([b3[:h], b2[h:]])
    total = ring_sums("z_hi", to_next, to_prev, (b1[:h], b3[h:]), (b0[:h], b0[h:]))
    total = jnp.concatenate(total, 0)

    own, near, far = pick(pos, slot_index, tokens, width)
    near = flip(near, "z_hi", 1)
    far = flip(jnp.concatenate([far, near[CAP:]], 0), "z_hi", 3)
    tok = jnp.concatenate([own, near[:CAP], far[CAP:], far[:CAP]], 0)[None]
    for bit in (4, 2, 1):
        tok = jnp.concatenate([tok, flip(tok, "z_lo", bit)], 0)
    tok = jnp.concatenate([tok] + [shift(tok, "y", s) for s in range(1, ny)], 0)
    tok = jnp.concatenate([tok] + [shift(tok, "core", s) for s in range(1, nc)], 0)
    tok = tok.reshape(-1, nx * width)

    average = total.reshape(width, 2, hid) / (nx * nz)
    new_first = 0.9 * moment1 + 0.1 * average
    new_second = 0.999 * moment2 + 0.001 * average * average
    correct_one = 1.0 - 0.9**STEP
    correct_two = 1.0 - 0.999**STEP
    ratio = new_first / correct_one / (jnp.sqrt(new_second / correct_two) + 1e-08)
    new_master = master - 0.001 * (ratio + 0.1 * master)
    own_w = new_master.astype(bf16).reshape(width, cols)
    ws = [own_w] + [shift(own_w, "x", s) for s in range(1, nx)]

    row = jnp.arange(tok.shape[0], dtype=jnp.int32)
    slot = row % CAP
    e = (row // CAP) % (ny * nl * nc)
    zt = row // (CAP * ny * nl * nc)
    ec, el, ey = e % nc, (e // nc) % nl, e // (nc * nl)
    dl = el ^ low
    dl = (dl >> 2) + (dl & 2) + 4 * (dl & 1)
    held = (((ec - core) % nc) * ny + (ey - y) % ny) * nl + dl
    where = held * (nz * CAP) + (zt ^ z) * CAP + slot
    pre = partial_pre(where[:, None], tok, ws).reshape(nz, -1, cols)
    pre = lax.all_to_all(pre, "z_hi", 0, 0, tiled=True)
    pre = jnp.sum(pre.astype(f32), axis=0)
    hidden = (jax.nn.silu(pre[:, :hid]) * pre[:, hid:]).astype(bf16)
    return (new_master, new_first, new_second, hidden[None])


def solution(mesh):
    sizes = (4, 8, 2, 4, 4) if mesh.shape["exp"] == 64 else (2, 4, 2, 4, 4)
    fine = Mesh(mesh.devices.reshape(sizes), ("y", "z_lo", "core", "x", "z_hi"))
    exp, rep = ("y", "z_lo", "core"), ("x", "z_hi")
    return jax.shard_map(
        compute,
        mesh=fine,
        in_specs=(
            P(exp + rep, None),
            P(exp + rep),
            P(rep, None, None),
            P(rep, None, None, exp),
            P(rep, None, exp),
            P(rep, None, exp),
            P(rep, None, exp),
        ),
        out_specs=(
            P(rep, None, exp),
            P(rep, None, exp),
            P(rep, None, exp),
            P(rep, None, exp),
        ),
        check_vma=False,
    )
```

```python
import functools

import jax
import jax.numpy as jnp
from jax import lax
from jax.experimental import pallas as pl
from jax.experimental.pallas import tpu as pltpu
from jax.sharding import Mesh, PartitionSpec as P


STEP = 100
CAP = 2
bf16, f32 = jnp.bfloat16, jnp.float32


def shift(a, axis, s):
    n = lax.axis_size(axis)
    return lax.ppermute(a, axis, [((i + s) % n, i) for i in range(n)])


def flip(a, axis, bit):
    n = lax.axis_size(axis)
    return lax.ppermute(a, axis, [(i, i ^ bit) for i in range(n)])


def grad_body(picks, pos, cot, *refs):
    n = len(picks)
    for saved, (_, m, half) in zip(refs[:n], picks):
        refs[n + m][half, 0] = jnp.dot(cot[...], saved[...], preferred_element_type=f32).astype(bf16)


def grad_blocks(pos, saved, cot, width, picks):
    cols, rows = cot.shape
    outs = 1 + max(m for _, m, _ in picks)

    def source(k, half):
        return lambda i, pos: (0, ((pos[0] + k) & 3) * 4 + ((pos[1] + 2 * half + i) & 3))

    return pl.pallas_call(
        functools.partial(grad_body, picks),
        grid_spec=pltpu.PrefetchScalarGridSpec(
            num_scalar_prefetch=1,
            grid=(2,),
            in_specs=[pl.BlockSpec((cols, rows), lambda i, pos: (0, 0))]
            + [pl.BlockSpec((rows, width), source(k, half)) for k, _, half in picks],
            out_specs=[pl.BlockSpec((2, 1, cols, width), lambda i, pos: (0, i, 0, 0))] * outs,
        ),
        out_shape=[jax.ShapeDtypeStruct((2, 2, cols, width), bf16)] * outs,
        name="grads",
    )(pos, cot, *[saved] * len(picks))


def pick_body(width, pos, slot, tok, own, near, far):
    t = tok.shape[0]
    row = lax.broadcasted_iota(jnp.int32, (t, 1), 0)
    hits = []
    for s in range(CAP):
        at = 0
        for i in range(t):
            at = at + jnp.where(slot[i] == s, i, 0)
        hits.append(row == at)
    for v, out, base in ((0, own, 0), (1, near, 0), (2, near, CAP), (3, far, 0)):
        for k in range(4):
            block = ((pos[0] + k) & 3) * 4 + (pos[1] ^ v)
            part = tok[:, pl.ds(pl.multiple_of(block * width, width), width)].astype(f32)
            rows = [jnp.sum(jnp.where(hit, part, 0.0), axis=0, keepdims=True) for hit in hits]
            out[base : base + CAP, k * width : (k + 1) * width] = jnp.concatenate(rows, 0).astype(bf16)


def pick(pos, slots, tokens, width):
    smem, vmem = pl.BlockSpec(memory_space=pltpu.SMEM), pl.BlockSpec(memory_space=pltpu.VMEM)
    return pl.pallas_call(
        functools.partial(pick_body, width),
        in_specs=[smem, smem, vmem],
        out_specs=[vmem] * 3,
        out_shape=[jax.ShapeDtypeStruct((n * CAP, 4 * width), bf16) for n in (1, 2, 1)],
        name="pick",
    )(pos, slots, tokens)


def pre_body(where, tok, w0, w1, w2, w3, out):
    width = w0.shape[0]
    acc = None
    for k, w in enumerate((w0, w1, w2, w3)):
        part = jnp.dot(tok[:, k * width : (k + 1) * width], w[...], preferred_element_type=f32)
        acc = part if acc is None else acc + part
    rows = acc.shape[0]
    source = where[...]
    perm = (source == lax.broadcasted_iota(jnp.int32, (rows, rows), 1)).astype(f32).astype(bf16)
    out[...] = jnp.dot(perm, acc.astype(bf16), preferred_element_type=f32).astype(bf16)


def partial_pre(where, tok, ws):
    rows, cols = tok.shape[0], ws[0].shape[1]
    vmem = pl.BlockSpec(memory_space=pltpu.VMEM)
    return pl.pallas_call(
        pre_body,
        in_specs=[vmem] * 6,
        out_specs=vmem,
        out_shape=jax.ShapeDtypeStruct((rows, cols), bf16),
        name="pre",
    )(where, tok, *ws)


def ring_sums(axis, to_next, to_prev, keep, mine):
    from_prev = shift(to_next, axis, -1)
    from_next = shift(to_prev, axis, 1)
    pass0 = add(keep[0], from_prev[0]).astype(bf16)
    pass1 = add(keep[1], from_next[1]).astype(bf16)
    more1 = shift(pass1, axis, 1)
    more0 = shift(pass0, axis, -1)
    return add(mine[0], from_next[0], more0), add(mine[1], from_prev[1], more1)


def add(*parts):
    total = parts[0].astype(f32)
    for part in parts[1:]:
        total = total + part.astype(f32)
    return total


def compute(tokens, slot_index, saved_inputs, cotangents, master, moment1, moment2):
    nx, nz = lax.axis_size("x"), lax.axis_size("z_hi")
    ny, nl, nc = lax.axis_size("y"), lax.axis_size("z_lo"), lax.axis_size("core")
    x, z = lax.axis_index("x"), lax.axis_index("z_hi")
    y, low, core = lax.axis_index("y"), lax.axis_index("z_lo"), lax.axis_index("core")
    saved = saved_inputs[0]
    cot = cotangents[0]
    hid = cot.shape[2]
    cols = 2 * hid
    cot = cot.reshape(cot.shape[0], cols).T
    width = saved.shape[1] // (nx * nz)

    pos = jnp.stack([x, z]).astype(jnp.int32)

    to_next, to_prev = grad_blocks(pos, saved, cot, width, [(2, 0, 0), (1, 0, 1), (3, 1, 0), (2, 1, 1)])
    keep, mine = grad_blocks(pos, saved, cot, width, [(1, 0, 0), (3, 0, 1), (0, 1, 0), (0, 1, 1)])
    near_sum, far_sum = ring_sums("x", to_next, to_prev, keep, mine)
    h = hid
    b0, b1 = near_sum[0], near_sum[1].astype(bf16)
    b2, b3 = far_sum[0].astype(bf16), far_sum[1].astype(bf16)
    to_next, to_prev = jnp.stack([b2[:h], b1[h:]]), jnp.stack([b3[:h], b2[h:]])
    total = ring_sums("z_hi", to_next, to_prev, (b1[:h], b3[h:]), (b0[:h], b0[h:]))
    total = jnp.stack([half.T for half in total], axis=1)

    own, near, far = pick(pos, slot_index, tokens, width)
    near = flip(near, "z_hi", 1)
    far = flip(jnp.concatenate([far, near[CAP:]], 0), "z_hi", 3)
    tok = jnp.concatenate([own, near[:CAP], far[CAP:], far[:CAP]], 0)[None]
    for bit in (4, 2, 1):
        tok = jnp.concatenate([tok, flip(tok, "z_lo", bit)], 0)
    tok = jnp.concatenate([tok] + [shift(tok, "y", s) for s in range(1, ny)], 0)
    tok = jnp.concatenate([tok] + [shift(tok, "core", s) for s in range(1, nc)], 0)
    tok = tok.reshape(-1, nx * width)

    average = total / (nx * nz)
    new_first = 0.9 * moment1 + 0.1 * average
    new_second = 0.999 * moment2 + 0.001 * average * average
    correct_one = 1.0 - 0.9**STEP
    correct_two = 1.0 - 0.999**STEP
    ratio = new_first / correct_one / (jnp.sqrt(new_second / correct_two) + 1e-08)
    new_master = master - 0.001 * (ratio + 0.1 * master)
    own_w = new_master.astype(bf16).reshape(width, cols)
    ws = [own_w] + [shift(own_w, "x", s) for s in range(1, nx)]

    row = jnp.arange(tok.shape[0], dtype=jnp.int32)
    slot = row % CAP
    e = (row // CAP) % (ny * nl * nc)
    zt = row // (CAP * ny * nl * nc)
    ec, el, ey = e % nc, (e // nc) % nl, e // (nc * nl)
    dl = el ^ low
    dl = (dl >> 2) + (dl & 2) + 4 * (dl & 1)
    held = (((ec - core) % nc) * ny + (ey - y) % ny) * nl + dl
    where = held * (nz * CAP) + (zt ^ z) * CAP + slot
    pre = partial_pre(where[:, None], tok, ws).reshape(nz, -1, cols)
    pre = lax.all_to_all(pre, "z_hi", 0, 0, tiled=True)
    pre = jnp.sum(pre.astype(f32), axis=0)
    hidden = (jax.nn.silu(pre[:, :hid]) * pre[:, hid:]).astype(bf16)
    return (new_master, new_first, new_second, hidden[None])


def solution(mesh):
    sizes = (4, 8, 2, 4, 4) if mesh.shape["exp"] == 64 else (2, 4, 2, 4, 4)
    fine = Mesh(mesh.devices.reshape(sizes), ("y", "z_lo", "core", "x", "z_hi"))
    exp, rep = ("y", "z_lo", "core"), ("x", "z_hi")
    return jax.shard_map(
        compute,
        mesh=fine,
        in_specs=(
            P(exp + rep, None),
            P(exp + rep),
            P(rep, None, None),
            P(rep, None, None, exp),
            P(rep, None, exp),
            P(rep, None, exp),
            P(rep, None, exp),
        ),
        out_specs=(
            P(rep, None, exp),
            P(rep, None, exp),
            P(rep, None, exp),
            P(rep, None, exp),
        ),
        check_vma=False,
    )
```

```python
import functools

import jax
import jax.numpy as jnp
from jax import lax
from jax.experimental import pallas as pl
from jax.experimental.pallas import tpu as pltpu
from jax.sharding import Mesh, PartitionSpec as P


STEP = 100
CAP = 2
bf16, f32 = jnp.bfloat16, jnp.float32


def shift(a, axis, s):
    n = lax.axis_size(axis)
    return lax.ppermute(a, axis, [((i + s) % n, i) for i in range(n)])


def flip(a, axis, bit):
    n = lax.axis_size(axis)
    return lax.ppermute(a, axis, [(i, i ^ bit) for i in range(n)])


def grad_body(picks, pos, cot, *refs):
    n = len(picks)
    for saved, (_, m, half) in zip(refs[:n], picks):
        block = lax.dot_general(saved[...], cot[...], (((0,), (0,)), ((), ())), preferred_element_type=f32)
        refs[n + m][half, 0] = block.astype(bf16)


def grad_blocks(pos, saved, cot, width, picks):
    rows, cols = cot.shape
    outs = 1 + max(m for _, m, _ in picks)

    def source(k, half):
        return lambda i, pos: (0, ((pos[0] + k) & 3) * 4 + ((pos[1] + 2 * half + i) & 3))

    return pl.pallas_call(
        functools.partial(grad_body, picks),
        grid_spec=pltpu.PrefetchScalarGridSpec(
            num_scalar_prefetch=1,
            grid=(2,),
            in_specs=[pl.BlockSpec((rows, cols), lambda i, pos: (0, 0))]
            + [pl.BlockSpec((rows, width), source(k, half)) for k, _, half in picks],
            out_specs=[pl.BlockSpec((2, 1, width, cols), lambda i, pos: (0, i, 0, 0))] * outs,
        ),
        out_shape=[jax.ShapeDtypeStruct((2, 2, width, cols), bf16)] * outs,
        name="grads",
    )(pos, cot, *[saved] * len(picks))


def pick_body(width, pos, slot, tok, own, near, far):
    t = tok.shape[0]
    row = lax.broadcasted_iota(jnp.int32, (t, 1), 0)
    hits = []
    for s in range(CAP):
        at = 0
        for i in range(t):
            at = at + jnp.where(slot[i] == s, i, 0)
        hits.append(row == at)
    for v, out, base in ((0, own, 0), (1, near, 0), (2, near, CAP), (3, far, 0)):
        for k in range(4):
            block = ((pos[0] + k) & 3) * 4 + (pos[1] ^ v)
            part = tok[:, pl.ds(pl.multiple_of(block * width, width), width)].astype(f32)
            rows = [jnp.sum(jnp.where(hit, part, 0.0), axis=0, keepdims=True) for hit in hits]
            out[base : base + CAP, k * width : (k + 1) * width] = jnp.concatenate(rows, 0).astype(bf16)


def pick(pos, slots, tokens, width):
    smem, vmem = pl.BlockSpec(memory_space=pltpu.SMEM), pl.BlockSpec(memory_space=pltpu.VMEM)
    return pl.pallas_call(
        functools.partial(pick_body, width),
        in_specs=[smem, smem, vmem],
        out_specs=[vmem] * 3,
        out_shape=[jax.ShapeDtypeStruct((n * CAP, 4 * width), bf16) for n in (1, 2, 1)],
        name="pick",
    )(pos, slots, tokens)


def pre_body(where, tok, w0, w1, w2, w3, out):
    width = w0.shape[0]
    acc = None
    for k, w in enumerate((w0, w1, w2, w3)):
        part = jnp.dot(tok[:, k * width : (k + 1) * width], w[...], preferred_element_type=f32)
        acc = part if acc is None else acc + part
    rows = acc.shape[0]
    source = where[...]
    perm = (source == lax.broadcasted_iota(jnp.int32, (rows, rows), 1)).astype(f32).astype(bf16)
    out[...] = jnp.dot(perm, acc.astype(bf16), preferred_element_type=f32).astype(bf16)


def partial_pre(where, tok, ws):
    rows, cols = tok.shape[0], ws[0].shape[1]
    vmem = pl.BlockSpec(memory_space=pltpu.VMEM)
    return pl.pallas_call(
        pre_body,
        in_specs=[vmem] * 6,
        out_specs=vmem,
        out_shape=jax.ShapeDtypeStruct((rows, cols), bf16),
        name="pre",
    )(where, tok, *ws)


def ring_sums(axis, to_next, to_prev, keep, mine):
    from_prev = shift(to_next, axis, -1)
    from_next = shift(to_prev, axis, 1)
    pass0 = add(keep[0], from_prev[0]).astype(bf16)
    pass1 = add(keep[1], from_next[1]).astype(bf16)
    more1 = shift(pass1, axis, 1)
    more0 = shift(pass0, axis, -1)
    return add(mine[0], from_next[0], more0), add(mine[1], from_prev[1], more1)


def add(*parts):
    total = parts[0].astype(f32)
    for part in parts[1:]:
        total = total + part.astype(f32)
    return total


def compute(tokens, slot_index, saved_inputs, cotangents, master, moment1, moment2):
    nx, nz = lax.axis_size("x"), lax.axis_size("z_hi")
    ny, nl, nc = lax.axis_size("y"), lax.axis_size("z_lo"), lax.axis_size("core")
    x, z = lax.axis_index("x"), lax.axis_index("z_hi")
    y, low, core = lax.axis_index("y"), lax.axis_index("z_lo"), lax.axis_index("core")
    saved = saved_inputs[0]
    cot = cotangents[0]
    hid = cot.shape[2]
    cols = 2 * hid
    cot = cot.reshape(cot.shape[0], cols)
    width = saved.shape[1] // (nx * nz)

    pos = jnp.stack([x, z]).astype(jnp.int32)

    to_next, to_prev = grad_blocks(pos, saved, cot, width, [(2, 0, 0), (1, 0, 1), (3, 1, 0), (2, 1, 1)])
    keep, mine = grad_blocks(pos, saved, cot, width, [(1, 0, 0), (3, 0, 1), (0, 1, 0), (0, 1, 1)])
    near_sum, far_sum = ring_sums("x", to_next, to_prev, keep, mine)
    h = width // 2
    b0, b1 = near_sum[0], near_sum[1].astype(bf16)
    b2, b3 = far_sum[0].astype(bf16), far_sum[1].astype(bf16)
    to_next, to_prev = jnp.stack([b2[:h], b1[h:]]), jnp.stack([b3[:h], b2[h:]])
    total = ring_sums("z_hi", to_next, to_prev, (b1[:h], b3[h:]), (b0[:h], b0[h:]))
    total = jnp.concatenate(total, 0)

    own, near, far = pick(pos, slot_index, tokens, width)
    near = flip(near, "z_hi", 1)
    far = flip(jnp.concatenate([far, near[CAP:]], 0), "z_hi", 3)
    tok = jnp.concatenate([own, near[:CAP], far[CAP:], far[:CAP]], 0)[None]
    for bit in (4, 2, 1):
        tok = jnp.concatenate([tok, flip(tok, "z_lo", bit)], 0)
    tok = jnp.concatenate([tok] + [shift(tok, "y", s) for s in range(1, ny)], 0)
    tok = jnp.concatenate([tok] + [shift(tok, "core", s) for s in range(1, nc)], 0)
    tok = tok.reshape(-1, nx * width)

    average = total.reshape(width, 2, hid) / (nx * nz)
    new_first = 0.9 * moment1 + 0.1 * average
    new_second = 0.999 * moment2 + 0.001 * average * average
    correct_one = 1.0 - 0.9**STEP
    correct_two = 1.0 - 0.999**STEP
    ratio = new_first / correct_one / (jnp.sqrt(new_second / correct_two) + 1e-08)
    new_master = master - 0.001 * (ratio + 0.1 * master)
    own_w = new_master.astype(bf16).reshape(width, cols)
    ws = [own_w] + [shift(own_w, "x", s) for s in range(1, nx)]

    row = jnp.arange(tok.shape[0], dtype=jnp.int32)
    slot = row % CAP
    e = (row // CAP) % (ny * nl * nc)
    zt = row // (CAP * ny * nl * nc)
    ec, el, ey = e % nc, (e // nc) % nl, e // (nc * nl)
    dl = el ^ low
    dl = (dl >> 2) + (dl & 2) + 4 * (dl & 1)
    held = (((ec - core) % nc) * ny + (ey - y) % ny) * nl + dl
    where = held * (nz * CAP) + (((zt + z) % nz) ^ z) * CAP + slot
    pre = partial_pre(where[:, None], tok, ws).reshape(nz, -1, cols)
    h = pre.shape[1] // 2
    to_next, to_prev = jnp.stack([pre[2, :h], pre[1, h:]]), jnp.stack([pre[3, :h], pre[2, h:]])
    pre = ring_sums("z_hi", to_next, to_prev, (pre[1, :h], pre[3, h:]), (pre[0, :h], pre[0, h:]))
    pre = jnp.concatenate(pre, 0)
    hidden = (jax.nn.silu(pre[:, :hid]) * pre[:, hid:]).astype(bf16)
    return (new_master, new_first, new_second, hidden[None])


def solution(mesh):
    sizes = (4, 8, 2, 4, 4) if mesh.shape["exp"] == 64 else (2, 4, 2, 4, 4)
    fine = Mesh(mesh.devices.reshape(sizes), ("y", "z_lo", "core", "x", "z_hi"))
    exp, rep = ("y", "z_lo", "core"), ("x", "z_hi")
    return jax.shard_map(
        compute,
        mesh=fine,
        in_specs=(
            P(exp + rep, None),
            P(exp + rep),
            P(rep, None, None),
            P(rep, None, None, exp),
            P(rep, None, exp),
            P(rep, None, exp),
            P(rep, None, exp),
        ),
        out_specs=(
            P(rep, None, exp),
            P(rep, None, exp),
            P(rep, None, exp),
            P(rep, None, exp),
        ),
        check_vma=False,
    )
```
